128 devices in a mesh: wide: 32 (over x, z, core), narrow: 4 (over y).
Axes of the slice: x: 4, y: 4, z: 4, core: 2. Of those that a mesh axis runs over, the one named last changes fastest.
Arguments:
- tokens: bfloat16 [4096, 3584], P(('wide', 'narrow')), may hold values from -6 to 6
- norm_gain: float32 [3584], replicated, may hold values from 0.1 to 1.9
- expert_ids: int32 [4096, 8], P(('wide', 'narrow')), may hold values from 0 to 127, all different within a row; in each aligned block of 32 rows (0 to 31, 32 to 63, ...) at most 3 rows name the same one
- gate_values: int32 [4096, 8], P(('wide', 'narrow')), may hold values from 1 to 65535
- w_gate: bfloat16 [128, 3584, 1024], P(('wide', 'narrow')), may hold values from -0.09375 to 0.09375
- w_up: bfloat16 [128, 3584, 1024], P(('wide', 'narrow')), may hold values from -0.09375 to 0.09375
- w_down: bfloat16 [128, 1024, 3584], P(('wide', 'narrow')), may hold values from -0.1875 to 0.1875
- queries: bfloat16 [256, 73728], P(('wide', 'narrow')), may hold values from -48 to 48
- latent_cache: bfloat16 [256, 589824], P(('wide', 'narrow')), may hold values from -8 to 8
- cache_lengths: int32 [256], P(('wide', 'narrow')), may hold values from 2 to 1024, as said below
Outputs:
- combined: bfloat16 [4096, 3584], P(('wide', 'narrow'))
- attention: bfloat16 [256, 65536], P(('wide', 'narrow'))
The draws below stay inside these ranges and needn't reach their ends.
Inputs may be any that keep to these rules, and one draw needn't show every extreme that they name: `expert_ids`: each row names 8 different experts; among the 32 rows of one device no expert is named more than 3 times, and some device's rows name some expert exactly 3 times. `cache_lengths`: some request has exactly 1024 cached positions.
All inputs are finite; a program needn't handle non-finite values.
Results may differ from the reference program's by a relative error of at most 0.0068.
Values may be sent and summed in bfloat16 or wider, within the bound.
No kernel may reach another device: no remote copies, remote signals or barrier semaphores. Data moves between devices by JAX's collectives and lax.ppermute only.
A program may use at most 128 MiB of HBM per device.

```python
import math
import jax
import jax.numpy as jnp
import numpy as np
from jax import lax

D = 3584
HID = 1024
HEADS = 128
LATENT = 512
QK = 576
TOP = 8
TOK_DEV = 32
CTX = 1024
EXPERTS = 128
CAP = 3
TOKENS = 4096
REQS = 256


def cache_values(key):
    values = jax.random.normal(jax.random.fold_in(key, 11), (REQS, CTX, QK), jnp.float32)
    return jnp.clip(values, -8.0, 8.0)


def draw_latent_cache(key, part):
    return cache_values(key).reshape(REQS, CTX * QK).astype(jnp.bfloat16)


def draw_queries(key, part):
    result = jax.random.normal(jax.random.fold_in(key, 21), (REQS, HEADS, QK), jnp.float32)
    result = jnp.clip(result, -6.0, 6.0)
    return jnp.clip(result, -48.0, 48.0).reshape(REQS, HEADS * QK).astype(jnp.bfloat16)


def draw_cache_lengths(key, part):
    base_lengths = jax.random.randint(jax.random.fold_in(key, 31), (REQS,), 2, CTX + 1)
    full_one = jax.random.randint(jax.random.fold_in(key, 32), (), 0, REQS)
    return jnp.where(jnp.arange(REQS) == full_one, CTX, base_lengths).astype(jnp.int32)


def with_ends(values, own_key, smallest, largest):
    longest = values.shape.index(max(values.shape))
    spots = []
    for shift in (0, 1):
        where = [jax.random.randint(jax.random.fold_in(own_key, axis), (), 0, length) for axis, length in enumerate(values.shape)]
        where[longest] = (where[longest] + shift) % values.shape[longest]
        spots.append(tuple(where))
    return values.at[spots[0]].set(smallest).at[spots[1]].set(largest)


def block_levels(stream_key, extent, split, least, largest):
    def one(dim, blocks):
        draws = jax.random.uniform(jax.random.fold_in(jax.random.fold_in(stream_key, 6), dim), (blocks,), jnp.float32, least / len(split), largest / len(split))
        return jnp.repeat(jnp.exp(draws), extent[dim] // blocks).reshape((-1,) + (1,) * (len(extent) - dim - 1))

    level = one(*split[0])
    for cut in split[1:]:
        level = level * one(*cut)
    return level


def routed_block(key, own, number, rows, amount, top, most, lean):
    sequence = jax.random.permutation(key, amount)
    crowded, usual = shares(amount, rows * top, most, lean, True), shares(amount, rows * top, most, lean, False)
    places = jnp.arange(amount)

    def named(tallies, rotation):
        used = int((tallies > 0).sum())
        fixed = max(1, used // 4)
        passed = fixed + (places - fixed + rotation * (used - fixed)) % max(1, amount - fixed)
        return jnp.zeros((amount,), jnp.int32).at[sequence[jnp.where(places < fixed, places, passed)]].set(jnp.asarray(tallies, jnp.int32))

    tallies = jnp.where(number % 4 == 0, named(crowded, number // 4), named(usual, number - number // 4 - 1))
    mixed = jax.random.permutation(jax.random.fold_in(own, 3), amount)
    giver, receiver = mixed[0:amount // 2 * 2:2], mixed[1:amount // 2 * 2:2]
    slack = jnp.minimum(tallies[giver] - 1, most - tallies[receiver]) // 2
    slack = jnp.where((giver == sequence[0]) | (receiver == sequence[0]) | (tallies[receiver] == 0), 0, jnp.maximum(slack, 0))
    passed = jax.random.randint(jax.random.fold_in(own, 4), (amount // 2,), 0, 1 << 20) % (slack + 1)
    tallies = tallies.at[giver].add(-passed).at[receiver].add(passed)
    members = jnp.searchsorted(jnp.cumsum(tallies), jnp.arange(rows * top), side="right").astype(jnp.int32)
    table = members.reshape(top, rows).T
    table = table[jax.random.permutation(jax.random.fold_in(own, 1), rows)]
    rotation = jax.random.randint(jax.random.fold_in(own, 2), (rows, 1), 0, top)
    return jnp.take_along_axis(table, (jnp.arange(top)[None, :] + rotation) % top, axis=1)


def shares(number_of, total, reach, lean, full):
    loads = [(1 << 20) // math.isqrt(grade ** lean) + 1 for grade in range(1, number_of + 1)]
    largest = reach if full else min(reach, max(-(-total // number_of), total * loads[0] // sum(loads)))
    least = 1 if total - largest >= number_of - 1 else 0
    given, spare = [largest] + [least] * (number_of - 1), total - largest - least * (number_of - 1)
    while spare > 0:
        free = [i for i in range(1, number_of) if given[i] < largest] or [i for i in range(1, number_of) if given[i] < reach]
        pool, left = sum([loads[i] for i in free]), spare
        for i in free:
            addition = min(reach - given[i], max(1, left * loads[i] // pool), spare)
            given[i] = given[i] + addition
            spare = spare - addition
    return np.array(given)


def scatter_about(rng, shape, spread, limit, pieces=(), kind=jnp.bfloat16):
    level = block_levels(rng, shape, pieces, -0.22, 0.18) if pieces else 1.0
    entries = jax.random.normal(rng, shape, jnp.float32) * spread * level
    return jnp.minimum(jnp.maximum(entries, -limit), limit).astype(kind)


def setup_inputs(seed: int = 0) -> dict:
    arg_keys = jax.random.split(jax.random.key(seed), 11)
    tokens = scatter_about(arg_keys[0], (TOKENS, D), 1.0, 6.0, ((0, 128),))
    norm_gain = jnp.clip(1.0 + 0.18 * jax.random.normal(arg_keys[1], (D,), jnp.float32), 0.1, 1.9)
    expert_ids_keys = jax.random.split(jax.random.fold_in(arg_keys[2], 1), TOKENS // TOK_DEV)
    expert_ids_turns = jax.random.permutation(jax.random.fold_in(arg_keys[2], 3), TOKENS // TOK_DEV)
    expert_ids = jax.vmap(lambda own, number: routed_block(jax.random.fold_in(arg_keys[2], 2), own, number, TOK_DEV, EXPERTS, TOP, CAP, 2))(expert_ids_keys, expert_ids_turns).reshape((TOKENS, TOP))
    gate_values = with_ends(jax.random.randint(arg_keys[3], (TOKENS, TOP), 1, 65536), jax.random.fold_in(arg_keys[3], 1), 1, 65535).astype(jnp.int32)
    w_gate = scatter_about(arg_keys[4], (EXPERTS, D, HID), D ** -0.5, 0.09375, ((0, 128),))
    w_up = scatter_about(arg_keys[5], (EXPERTS, D, HID), D ** -0.5, 0.09375, ((0, 128),))
    w_down = scatter_about(arg_keys[6], (EXPERTS, HID, D), HID ** -0.5, 0.1875, ((0, 128),))
    queries = draw_queries(jax.random.fold_in(arg_keys[10], 71), 0)
    latent_cache = draw_latent_cache(jax.random.fold_in(arg_keys[10], 71), 0)
    cache_lengths = draw_cache_lengths(jax.random.fold_in(arg_keys[10], 71), 0)
    return dict(tokens=tokens, norm_gain=norm_gain, expert_ids=expert_ids, gate_values=gate_values, w_gate=w_gate, w_up=w_up, w_down=w_down, queries=queries, latent_cache=latent_cache, cache_lengths=cache_lengths)


score_scale = 192.0 ** (-0.5)
norm_eps = 1e-06
gate_unit = 32768.0

def attend_one(inputs):
    query_rows, cache_rows, length_one = inputs
    query_block = query_rows.reshape(HEADS, QK)
    cache_block = cache_rows.reshape(CTX, QK)
    scores = jnp.dot(query_block, cache_block.T, preferred_element_type=jnp.float32) * score_scale
    visible = jnp.arange(CTX, dtype=jnp.int32)[None, :] < length_one
    scores = jnp.where(visible, scores, -jnp.inf)
    peak = lax.optimization_barrier(jnp.max(scores, axis=1, keepdims=True))
    weights = jnp.exp(scores - peak)
    weights = (weights / lax.optimization_barrier(jnp.sum(weights, axis=1, keepdims=True))).astype(jnp.bfloat16)
    mixed = jnp.dot(weights, cache_block[:, :LATENT], preferred_element_type=jnp.float32)
    return mixed.astype(jnp.bfloat16).reshape(HEADS * LATENT)

def reference(tokens, norm_gain, expert_ids, gate_values, w_gate, w_up, w_down, queries, latent_cache, cache_lengths):
    attention = lax.map(attend_one, (queries, latent_cache, cache_lengths))
    token_float = tokens.astype(jnp.float32)
    squares = lax.optimization_barrier(jnp.mean(token_float * token_float, axis=1, keepdims=True))
    normed = (token_float * lax.rsqrt(squares + norm_eps) * norm_gain).astype(jnp.bfloat16)
    flat_ids = expert_ids.reshape(-1).astype(jnp.int32)
    pairs_count = TOKENS * TOP
    order = jnp.argsort(flat_ids, stable=True).astype(jnp.int32)
    expert_range = jnp.arange(EXPERTS, dtype=jnp.int32)
    counts = lax.optimization_barrier(jnp.sum((flat_ids[:, None] == expert_range[None, :]).astype(jnp.int32), axis=0))
    starts = jnp.cumsum(counts) - counts
    most_rows = EXPERTS * CAP

    def one_expert(inputs):
        expert, gate_matrix, up_matrix, down_matrix = inputs
        offsets = jnp.arange(most_rows, dtype=jnp.int32)
        usable = offsets < counts[expert]
        picks = order[jnp.minimum(starts[expert] + offsets, pairs_count - 1)]
        rows_in = jnp.where(usable[:, None], normed[picks // TOP], jnp.zeros((), jnp.bfloat16))
        gate_part = jnp.dot(rows_in, gate_matrix, preferred_element_type=jnp.float32)
        up_part = jnp.dot(rows_in, up_matrix, preferred_element_type=jnp.float32)
        inner = (jax.nn.silu(gate_part) * up_part).astype(jnp.bfloat16)
        outputs = jnp.dot(inner, down_matrix, preferred_element_type=jnp.float32).astype(jnp.bfloat16)
        places = jnp.where(usable, picks, pairs_count).astype(jnp.int32)
        return (places, outputs)
    places, outputs = lax.map(one_expert, (expert_range, w_gate, w_up, w_down))
    pair_out = jnp.zeros((pairs_count + 1, D), jnp.bfloat16)
    pair_out = pair_out.at[places.reshape(-1)].set(outputs.reshape(-1, D))[:pairs_count]
    gate_weights = gate_values.astype(jnp.float32) / gate_unit
    expert_sum = lax.optimization_barrier(jnp.sum(gate_weights[:, :, None] * pair_out.reshape(TOKENS, TOP, D).astype(jnp.float32), axis=1))
    combined = (token_float + expert_sum).astype(jnp.bfloat16)
    return (combined, attention)
```

```python
import jax
import jax.numpy as jnp
from jax import lax
from jax.experimental import pallas as pl
from jax.experimental.pallas import tpu as pltpu
from jax.sharding import PartitionSpec as P

HEADS = 128
LATENT = 512
QK = 576
TOP = 8
CTX = 1024
WIDTH = 3584
HID = 1024
EXPERTS = 128
ROWS = 32
SLOTS = 3
PACK = 8
LANES = 1408
HEAD = 2 * LANES
TAIL = ((0, 2816, 768, 6, 0), (1, 2816, 640, 6, 768), (1, 3456, 128, 7, 768), (2, 2816, 768, 7, 0))
BLOCK = 256
BLOCKS = EXPERTS * PACK // BLOCK
PEERS = BLOCK // PACK
GU_TILE = 256
D_TILE = 512

score_scale = 192.0 ** (-0.5)
norm_eps = 1e-06
gate_unit = 32768.0


def attend_local(queries, latent_cache, cache_lengths):
    requests = queries.shape[0]
    query_block = queries.reshape(requests, HEADS, QK)
    cache_block = latent_cache.reshape(requests, CTX, QK)
    scores = (
        jnp.einsum("rhq,rtq->rht", query_block, cache_block, preferred_element_type=jnp.float32)
        * score_scale
    )
    visible = jnp.arange(CTX, dtype=jnp.int32)[None, None, :] < cache_lengths[:, None, None]
    scores = jnp.where(visible, scores, -jnp.inf)
    peak = jnp.max(scores, axis=2, keepdims=True)
    weights = jnp.exp(scores - peak)
    weights = (weights / jnp.sum(weights, axis=2, keepdims=True)).astype(jnp.bfloat16)
    mixed = jnp.einsum(
        "rht,rtl->rhl", weights, cache_block[:, :, :LATENT], preferred_element_type=jnp.float32
    )
    return mixed.astype(jnp.bfloat16).reshape(requests, HEADS * LATENT)


def dot(left, right):
    return jnp.dot(left, right, preferred_element_type=jnp.float32)


def spread_matrix():
    row = lax.broadcasted_iota(jnp.int32, (BLOCK, BLOCK), 0)
    col = lax.broadcasted_iota(jnp.int32, (BLOCK, BLOCK), 1)
    return (col == (row % PACK) * PEERS + row // PACK).astype(jnp.float32).astype(jnp.bfloat16)


def collect_matrix():
    row = lax.broadcasted_iota(jnp.int32, (BLOCK, BLOCK), 0)
    col = lax.broadcasted_iota(jnp.int32, (BLOCK, BLOCK), 1)
    return (row == (col % PACK) * PEERS + col // PACK).astype(jnp.float32).astype(jnp.bfloat16)


def pack_rows(rows_ref, stage_ref, out_ref):
    spread = spread_matrix()
    for b in range(BLOCKS):
        base = b * BLOCK

        def rows_of(slot, first, count):
            start = slot * EXPERTS + b * PEERS
            return rows_ref[start : start + PEERS, first : first + count]

        for slot in range(SLOTS):
            for half in range(2):
                at = base + (2 * slot + half) * PEERS
                stage_ref[at : at + PEERS, :] = rows_of(slot, half * LANES, LANES)
        for slot, first, count, row, lane in TAIL:
            at = base + row * PEERS
            stage_ref[at : at + PEERS, lane : lane + count] = rows_of(slot, first, count)
        at = base + 7 * PEERS
        stage_ref[at : at + PEERS, 896:LANES] = jnp.zeros((PEERS, LANES - 896), jnp.bfloat16)
        out_ref[base : base + BLOCK, :] = dot(spread, stage_ref[base : base + BLOCK, :]).astype(
            jnp.bfloat16
        )


def unpack_rows(in_ref, rows_ref):
    collect = collect_matrix()
    for b in range(BLOCKS):
        base = b * BLOCK
        block = dot(collect, in_ref[base : base + BLOCK, :]).astype(jnp.bfloat16)

        def put(slot, first, count, row, lane):
            start = slot * EXPERTS + b * PEERS
            rows_ref[start : start + PEERS, first : first + count] = block[
                row * PEERS : (row + 1) * PEERS, lane : lane + count
            ]

        for slot in range(SLOTS):
            for half in range(2):
                put(slot, half * LANES, LANES, 2 * slot + half, 0)
        for slot, first, count, row, lane in TAIL:
            put(slot, first, count, row, lane)


def dispatch_kernel(tokens_ref, gain_ref, ids_ref, out_ref, rows_ref, stage_ref):
    token_float = tokens_ref[...].astype(jnp.float32)
    squares = jnp.mean(token_float * token_float, axis=1, keepdims=True)
    normed = (token_float * lax.rsqrt(squares + norm_eps) * gain_ref[...]).astype(jnp.bfloat16)
    expert = lax.broadcasted_iota(jnp.int32, (EXPERTS, ROWS), 0)
    named = jnp.zeros((EXPERTS, ROWS), jnp.float32)
    for k in range(TOP):
        named = named + (ids_ref[k : k + 1, :] == expert).astype(jnp.float32)
    earlier = (
        lax.broadcasted_iota(jnp.int32, (ROWS, ROWS), 0)
        < lax.broadcasted_iota(jnp.int32, (ROWS, ROWS), 1)
    ).astype(jnp.float32)
    rank = dot(named.astype(jnp.bfloat16), earlier.astype(jnp.bfloat16))
    for slot in range(SLOTS):
        pick = jnp.where(rank == float(slot), named, 0.0).astype(jnp.bfloat16)
        rows_ref[slot * EXPERTS : (slot + 1) * EXPERTS, :] = dot(pick, normed).astype(jnp.bfloat16)
    pack_rows(rows_ref, stage_ref, out_ref)


def expert_kernel(
    in_ref, gate_hbm, up_hbm, down_hbm, out_ref,
    rows_ref, inner_ref, stage_ref, gate_ref, up_ref, down_ref, gate_sem, up_sem, down_sem,
):
    gu_tiles = HID // GU_TILE
    d_tiles = WIDTH // D_TILE

    def gate_copy(h):
        cols = pl.ds(h * GU_TILE, GU_TILE)
        return pltpu.make_async_copy(gate_hbm.at[0, :, cols], gate_ref.at[h], gate_sem.at[h])

    def up_copy(h):
        cols = pl.ds(h * GU_TILE, GU_TILE)
        return pltpu.make_async_copy(up_hbm.at[0, :, cols], up_ref.at[h], up_sem.at[h])

    def down_copy(d):
        cols = pl.ds(d * D_TILE, D_TILE)
        return pltpu.make_async_copy(down_hbm.at[0, :, cols], down_ref.at[d], down_sem.at[d])

    for h in range(gu_tiles):
        gate_copy(h).start()
        up_copy(h).start()
    for d in range(d_tiles):
        down_copy(d).start()
    unpack_rows(in_ref, rows_ref)
    for h in range(gu_tiles):
        gate_copy(h).wait()
        gate_part = dot(rows_ref[...], gate_ref[h])
        up_copy(h).wait()
        up_part = dot(rows_ref[...], up_ref[h])
        inner = gate_part / (1.0 + jnp.exp(-gate_part)) * up_part
        inner_ref[:, h * GU_TILE : (h + 1) * GU_TILE] = inner.astype(jnp.bfloat16)
    for d in range(d_tiles):
        down_copy(d).wait()
        rows_ref[:, d * D_TILE : (d + 1) * D_TILE] = dot(inner_ref[...], down_ref[d]).astype(
            jnp.bfloat16
        )
    pack_rows(rows_ref, stage_ref, out_ref)


def combine_kernel(in_ref, tokens_ref, ids_ref, values_ref, out_ref, rows_ref):
    expert = lax.broadcasted_iota(jnp.int32, (ROWS, EXPERTS), 1)
    named = jnp.zeros((ROWS, EXPERTS), jnp.float32)
    value = jnp.zeros((ROWS, EXPERTS), jnp.int32)
    for k in range(TOP):
        hit = ids_ref[:, k : k + 1] == expert
        named = named + hit.astype(jnp.float32)
        value = value + jnp.where(hit, values_ref[:, k : k + 1], 0)
    later = (
        lax.broadcasted_iota(jnp.int32, (ROWS, ROWS), 1)
        < lax.broadcasted_iota(jnp.int32, (ROWS, ROWS), 0)
    ).astype(jnp.float32)
    rank = dot(later.astype(jnp.bfloat16), named.astype(jnp.bfloat16))
    high = (value // 256).astype(jnp.float32) * (256.0 / gate_unit)
    low = (value % 256).astype(jnp.float32) * (1.0 / gate_unit)
    both = jnp.concatenate([high, low], axis=0)
    rank = jnp.concatenate([rank, rank], axis=0)
    unpack_rows(in_ref, rows_ref)
    total = jnp.zeros((2 * ROWS, WIDTH), jnp.float32)
    for slot in range(SLOTS):
        weight = jnp.where(rank == float(slot), both, 0.0).astype(jnp.bfloat16)
        total = total + dot(weight, rows_ref[slot * EXPERTS : (slot + 1) * EXPERTS, :])
    token_float = tokens_ref[...].astype(jnp.float32)
    out_ref[...] = (token_float + (total[:ROWS] + total[ROWS:])).astype(jnp.bfloat16)


def vmem():
    return pl.BlockSpec(memory_space=pltpu.VMEM)


def hbm():
    return pl.BlockSpec(memory_space=pl.ANY)


def params(mebibytes):
    return pltpu.CompilerParams(vmem_limit_bytes=mebibytes * 1024 * 1024)


packed_shape = jax.ShapeDtypeStruct((EXPERTS * PACK, LANES), jnp.bfloat16)
rows_scratch = pltpu.VMEM((SLOTS * EXPERTS, WIDTH), jnp.bfloat16)
stage_scratch = pltpu.VMEM((EXPERTS * PACK, LANES), jnp.bfloat16)


def exchange(packed):
    blocks = packed.reshape(EXPERTS, PACK, LANES)
    moved = lax.all_to_all(blocks, ("wide", "narrow"), split_axis=0, concat_axis=0, tiled=True)
    return moved.reshape(EXPERTS * PACK, LANES)


def on_device(
    tokens,
    norm_gain,
    expert_ids,
    gate_values,
    w_gate,
    w_up,
    w_down,
    queries,
    latent_cache,
    cache_lengths,
):
    attention = attend_local(queries, latent_cache, cache_lengths)
    packed = pl.pallas_call(
        dispatch_kernel,
        out_shape=packed_shape,
        in_specs=[vmem(), vmem(), vmem()],
        out_specs=vmem(),
        scratch_shapes=[rows_scratch, stage_scratch],
        compiler_params=params(24),
        name="dispatch",
    )(tokens, norm_gain.reshape(1, WIDTH), expert_ids.T)
    arrived = exchange(packed)
    worked = pl.pallas_call(
        expert_kernel,
        out_shape=packed_shape,
        in_specs=[vmem(), hbm(), hbm(), hbm()],
        out_specs=vmem(),
        scratch_shapes=[
            rows_scratch,
            pltpu.VMEM((SLOTS * EXPERTS, HID), jnp.bfloat16),
            stage_scratch,
            pltpu.VMEM((HID // GU_TILE, WIDTH, GU_TILE), jnp.bfloat16),
            pltpu.VMEM((HID // GU_TILE, WIDTH, GU_TILE), jnp.bfloat16),
            pltpu.VMEM((WIDTH // D_TILE, HID, D_TILE), jnp.bfloat16),
            pltpu.SemaphoreType.DMA((HID // GU_TILE,)),
            pltpu.SemaphoreType.DMA((HID // GU_TILE,)),
            pltpu.SemaphoreType.DMA((WIDTH // D_TILE,)),
        ],
        compiler_params=params(48),
        name="experts",
    )(arrived, w_gate, w_up, w_down)
    returned = exchange(worked)
    combined = pl.pallas_call(
        combine_kernel,
        out_shape=jax.ShapeDtypeStruct(tokens.shape, jnp.bfloat16),
        in_specs=[vmem(), vmem(), vmem(), vmem()],
        out_specs=vmem(),
        scratch_shapes=[rows_scratch],
        compiler_params=params(24),
        name="combine",
    )(returned, tokens, expert_ids, gate_values)
    return (combined, attention)


def solution(mesh):
    in_specs = (
        P(("wide", "narrow"), None),
        P(),
        P(("wide", "narrow"), None),
        P(("wide", "narrow"), None),
        P(("wide", "narrow"), None, None),
        P(("wide", "narrow"), None, None),
        P(("wide", "narrow"), None, None),
        P(("wide", "narrow"), None),
        P(("wide", "narrow"), None),
        P(("wide", "narrow")),
    )
    out_specs = (P(("wide", "narrow"), None), P(("wide", "narrow"), None))
    return jax.shard_map(
        on_device, mesh=mesh, in_specs=in_specs, out_specs=out_specs, check_vma=False
    )
```
